32 devices in a mesh: gx: 4 (over z), gy: 4 (over x, core), gz: 2 (over y).
Axes of the slice: x: 2, y: 2, z: 4, core: 2. Of those that a mesh axis runs over, the one named last changes fastest.
Arguments:
- right_sides: float32 [2, 32, 1024, 1024], P(None, ('gx', 'gy', 'gz')), may hold values from -6 to 6
- projector: float32 [2, 32, 1024, 192], P(None, ('gx', 'gy', 'gz')), may hold values from -0.1875 to 0.1875
- mixing: float32 [6, 2, 32, 2, 192, 192], P(None, None, ('gx', 'gy', 'gz')), may hold values from -0.3125 to 0.3125
- expander: float32 [64, 1024, 192], P(('gx', 'gy', 'gz')), may hold values from -0.4375 to 0.4375
Outputs:
- product: float32 [64, 1024, 1024], P(('gx', 'gy', 'gz'))
The draws below stay inside these ranges and needn't reach their ends.
All inputs are finite; a program needn't handle non-finite values.
Results may differ from the reference program's by a relative error of at most 0.0001.
Values sent between devices are 32-bit elements; how exact they have to be, the bound alone decides.
A program may use at most 128 MiB of HBM per device.

```python
import jax
import jax.numpy as jnp
from jax import lax

LEAF = 1024
K = 192
RHS = 1024
NODES = 64
LEVELS = 6
DEVICES = 32


def levels(key, dims, pieces, smallest, top_value):
    gain = 1.0
    for position, blocks in pieces:
        draws = jax.random.uniform(jax.random.fold_in(jax.random.fold_in(key, 6), position), (blocks,), jnp.float32, smallest / len(pieces), top_value / len(pieces))
        gain = gain * jnp.repeat(jnp.exp(draws), dims[position] // blocks).reshape((-1,) + (1,) * (len(dims) - 1 - position))
    return gain


def scatter_about(key, extent, spread, limit, split=(), held_as=jnp.bfloat16):
    array = spread * jax.random.normal(key, extent, jnp.float32)
    if split:
        array = array * levels(key, extent, split, -0.22, 0.18)
    return jnp.clip(array, -limit, limit).astype(held_as)


def setup_inputs(seed: int = 0) -> dict:
    splits = jax.random.split(jax.random.key(seed), 5)
    return {
        "right_sides": scatter_about(splits[0], (2, DEVICES, LEAF, RHS), 1.0, 6.0, ((1, 32),), jnp.float32),
        "projector": scatter_about(splits[1], (2, DEVICES, LEAF, K), LEAF ** -0.5, 0.1875, ((1, 32),), jnp.float32),
        "mixing": scatter_about(splits[2], (LEVELS, 2, DEVICES, 2, K, K), (2 * K) ** -0.5, 0.3125, ((2, 32),), jnp.float32),
        "expander": scatter_about(splits[3], (NODES, LEAF, K), K ** -0.5, 0.4375, ((0, 32),), jnp.float32),
    }


exact = lax.Precision.HIGHEST


def mix_level(weights, coeffs, partner):
    local_term = jnp.einsum("nkj,njr->nkr", weights[:, 0], coeffs, precision=exact)
    remote_term = jnp.einsum("nkj,njr->nkr", weights[:, 1], partner, precision=exact)
    return local_term + remote_term


def reference(right_sides, projector, mixing, expander):
    leaf_data = right_sides.reshape(NODES, LEAF, RHS)
    leaf_proj = projector.reshape(NODES, LEAF, K)
    leaf_mix = mixing.reshape(LEVELS, NODES, 2, K, K)
    coeffs = jnp.einsum("nlk,nlr->nkr", leaf_proj, leaf_data, precision=exact)
    for level_index in range(LEVELS):
        stride = 2 ** level_index
        paired = coeffs.reshape(NODES // (2 * stride), 2, stride, K, RHS)
        partner = paired[:, ::-1].reshape(NODES, K, RHS)
        coeffs = mix_level(leaf_mix[level_index], coeffs, partner)
    bit_view = coeffs.reshape((2,) * LEVELS + (K, RHS))
    axis_order = tuple(range(LEVELS - 1, -1, -1)) + (LEVELS, LEVELS + 1)
    reordered = bit_view.transpose(axis_order).reshape(NODES, K, RHS)
    return jnp.einsum("nlk,nkr->nlr", expander, reordered, precision=exact)
```

```python
import functools

import jax
import jax.numpy as jnp
from jax import lax
from jax.experimental import pallas as pl
from jax.sharding import PartitionSpec as P


AXES = ("gx", "gy", "gz")
CHUNKS = 4


def dot3(eq, a, b):
    return jnp.einsum(eq, a, b, precision=lax.Precision.HIGH)


def split(x):
    hi = x.astype(jnp.bfloat16)
    lo = (x - hi.astype(jnp.float32)).astype(jnp.bfloat16)
    return hi, lo


def expand_kernel(e_ref, c_ref, *rest):
    o_ref = rest[-1]
    e_hi, e_lo = split(e_ref[0])
    c_hi, c_lo = split(c_ref[0])
    dot = functools.partial(jnp.dot, preferred_element_type=jnp.float32)
    o_ref[0] = dot(e_hi, c_hi) + (dot(e_hi, c_lo) + dot(e_lo, c_hi))


def expand(expander, coeffs, out, column_block, total):
    nodes, leaf, k = expander.shape
    width = coeffs.shape[2]
    rows = leaf
    in_specs = [
        pl.BlockSpec((1, rows, k), lambda n, i: (n, i, 0)),
        pl.BlockSpec((1, k, width), lambda n, i: (n, 0, 0)),
    ]
    operands = [expander, coeffs]
    aliases = {}
    if out is not None:
        in_specs.append(pl.BlockSpec(memory_space=pl.ANY))
        operands.append(out)
        aliases = {2: 0}
    return pl.pallas_call(
        expand_kernel,
        grid=(nodes, leaf // rows),
        in_specs=in_specs,
        out_specs=pl.BlockSpec((1, rows, width), lambda n, i: (n, i, column_block)),
        out_shape=jax.ShapeDtypeStruct((nodes, leaf, total), jnp.float32),
        input_output_aliases=aliases,
        cost_estimate=pl.CostEstimate(
            flops=6 * nodes * leaf * k * width,
            bytes_accessed=4 * nodes * (leaf * k + k * width + leaf * width),
            transcendentals=0,
        ),
    )(*operands)


def permuted(value, bits, where):
    return lax.ppermute(value, AXES, [(d, where(d)) for d in range(2**bits)])


def swap_local(value, bits, bit):
    own = jnp.right_shift(lax.axis_index(AXES), bit) % 2
    zero = own == 0
    arrived = permuted(jnp.where(zero, value[1], value[0]), bits, lambda d: d ^ (1 << bit))
    return jnp.stack([jnp.where(zero, value[0], arrived), jnp.where(zero, arrived, value[1])])


def mixed(weights, coeffs, partner):
    return dot3("nkj,njr->nkr", weights[:, 0], coeffs) + dot3(
        "nkj,njr->nkr", weights[:, 1], partner
    )


def shards(right_sides, projector, mixing, expander):
    data = right_sides[:, 0]
    proj = projector[:, 0]
    mix = mixing[:, :, 0]
    bits = lax.axis_size(AXES).bit_length() - 1
    top = bits - 1
    columns = data.shape[2]
    width = columns // CHUNKS

    def swap_ends(d):
        first, last = d & 1, (d >> top) & 1
        return (d & ~(1 | (1 << top))) | (first << top) | last

    def reverse_middle(d):
        middle = sum(((d >> b) & 1) << (top - b) for b in range(1, top))
        return (d & (1 | (1 << top))) | middle

    early = swap_local(mix[top], bits, 0)
    top_weights = swap_local(early, bits, top)
    last_weights = permuted(mix[bits], bits, swap_ends)

    moved = []
    for i in range(CHUNKS):
        coeffs = jnp.einsum(
            "nlk,nlr->nkr",
            proj,
            data[:, :, i * width : (i + 1) * width],
            precision=lax.Precision.HIGHEST,
        )
        for level in range(top):
            partner = permuted(coeffs, bits, lambda d: d ^ (1 << level))
            coeffs = mixed(mix[level], coeffs, partner)
        coeffs = swap_local(coeffs, bits, 0)
        coeffs = swap_local(coeffs, bits, top)
        coeffs = mixed(top_weights, coeffs, coeffs[::-1])
        coeffs = swap_local(coeffs, bits, 0)
        coeffs = mixed(last_weights, coeffs, coeffs[::-1])
        moved.append(permuted(coeffs, bits, reverse_middle))
    out = None
    for i, coeffs in enumerate(moved):
        out = expand(expander, coeffs, out, i, columns)
    return out


def solution(mesh):
    placed = (
        P(None, AXES, None, None),
        P(None, AXES, None, None),
        P(None, None, AXES, None, None, None),
        P(AXES, None, None),
    )
    return jax.shard_map(
        shards, mesh=mesh, in_specs=placed, out_specs=P(AXES, None, None), check_vma=False
    )
```

```python
import functools

import jax
import jax.numpy as jnp
from jax import lax
from jax.experimental import pallas as pl
from jax.experimental.pallas import tpu as pltpu
from jax.sharding import PartitionSpec as P

AXES = ("gx", "gy", "gz")
CHUNKS = 4


def split(x):
    hi = x.astype(jnp.bfloat16)
    lo = (x - hi.astype(jnp.float32)).astype(jnp.bfloat16)
    return hi, lo


def product(a, b):
    dot = functools.partial(jnp.dot, preferred_element_type=jnp.float32)
    return dot(a[0], b[0]) + (dot(a[0], b[1]) + dot(a[1], b[0]))


def expand_kernel(e_ref, c_ref, o_ref):
    o_ref[0] = product(split(e_ref[0]), split(c_ref[0, 0]))


def expand(expander, coeffs):
    nodes, leaf, k = expander.shape
    chunks, _, _, width = coeffs.shape
    return pl.pallas_call(
        expand_kernel,
        grid=(nodes, chunks),
        in_specs=[
            pl.BlockSpec((1, leaf, k), lambda n, c: (n, 0, 0)),
            pl.BlockSpec((1, 1, k, width), lambda n, c: (c, n, 0, 0)),
        ],
        out_specs=pl.BlockSpec((1, leaf, width), lambda n, c: (n, 0, c)),
        out_shape=jax.ShapeDtypeStruct((nodes, leaf, chunks * width), jnp.float32),
    )(expander, coeffs)


def butterfly_kernel(sizes, x_ref, mix_ref, o_ref, *scratch):
    bits = sum(size.bit_length() - 1 for size in sizes)
    top = bits - 1
    arrived = scratch[:top]
    values = (x_ref,) + tuple(scratch[top : 2 * top])
    (
        swap_a, swap_b, paired, swap_c, final, landed,
        early, w_top, w_last, send, recv, w_send, w_recv,
    ) = scratch[2 * top :]
    chunks = x_ref.shape[0]
    coords = [lax.axis_index(name) for name in AXES]
    me = (coords[0] * sizes[1] + coords[1]) * sizes[2] + coords[2]

    def bit_of(b):
        return (me // (1 << b)) % 2

    def place(d):
        return {
            "gx": d // (sizes[1] * sizes[2]),
            "gy": (d // sizes[2]) % sizes[1],
            "gz": d % sizes[2],
        }

    flips = [me + (1 - 2 * bit_of(b)) * (1 << b) for b in range(bits)]
    first, last = bit_of(0), bit_of(top)
    ends = me + (last - first) - (last - first) * (1 << top)
    middle = first + last * (1 << top)
    for b in range(1, top):
        middle = middle + bit_of(b) * (1 << (top - b))
    ends_move = first != last
    middle_move = middle != me

    def remote(src, dst, sems, index, target):
        return pltpu.make_async_remote_copy(
            src_ref=src,
            dst_ref=dst,
            send_sem=sems[0].at[index],
            recv_sem=sems[1].at[index],
            device_id=place(target),
            device_id_type=pl.DeviceIdType.MESH,
        )

    def transfer(stage, c):
        index = (stage, c)
        sems = (send, recv)
        if stage < top:
            return remote(values[stage].at[c], arrived[stage].at[c], sems, index, flips[stage])
        if stage == top:
            return remote(
                values[top].at[c, 1 - first], swap_a.at[c, first], sems, index, flips[0]
            )
        if stage == top + 1:
            return remote(swap_a.at[c, 1 - last], swap_b.at[c, last], sems, index, flips[top])
        if stage == top + 2:
            return remote(paired.at[c, 1 - first], swap_c.at[c, first], sems, index, flips[0])
        return remote(final.at[c], landed.at[c], sems, index, middle)

    w_sems = (w_send, w_recv)
    move_a = remote(mix_ref.at[top, 1 - first], early.at[first], w_sems, 0, flips[0])
    move_b = remote(mix_ref.at[bits], w_last, w_sems, 1, ends)
    move_c = remote(early.at[1 - last], w_top.at[last], w_sems, 2, flips[top])

    def mixed(weights, own, other, out):
        parts = [split(own[n]) for n in range(2)]
        others = parts[::-1] if other is None else [split(other[n]) for n in range(2)]
        for n in range(2):
            out[n] = product(split(weights[n, 0]), parts[n]) + product(
                split(weights[n, 1]), others[n]
            )

    barrier = pltpu.get_barrier_semaphore()
    for target in flips:
        pl.semaphore_signal(
            barrier, inc=1, device_id=place(target), device_id_type=pl.DeviceIdType.MESH
        )
    for moves, target in ((ends_move, ends), (middle_move, middle)):

        @pl.when(moves)
        def _():
            pl.semaphore_signal(
                barrier, inc=1, device_id=place(target), device_id_type=pl.DeviceIdType.MESH
            )

    moving = ends_move.astype(jnp.int32) + middle_move.astype(jnp.int32)
    pl.semaphore_wait(barrier, len(flips) + moving)

    def task(stage, c):
        if stage > 0:
            before = transfer(stage - 1, c)
            if stage - 1 == top + 3:
                pl.when(middle_move)(before.wait_recv)
            else:
                before.wait_recv()
        if 0 < stage <= top:
            mixed(
                mix_ref.at[stage - 1],
                values[stage - 1].at[c],
                arrived[stage - 1].at[c],
                values[stage].at[c],
            )
        if stage == top:
            swap_a[c, first] = values[top][c, first]
        if stage == top + 1:
            swap_b[c, last] = swap_a[c, last]
        if stage == top + 2:

            @pl.when(c == 0)
            def _():
                move_c.wait_recv()

            mixed(w_top, swap_b.at[c], None, paired.at[c])
            swap_c[c, first] = paired[c, first]
        if stage == top + 3:

            @pl.when((c == 0) & ends_move)
            def _():
                move_b.wait_recv()

            mixed(w_last, swap_c.at[c], None, final.at[c])
            pl.when(middle_move)(transfer(stage, c).start)
        elif stage < top + 3:
            transfer(stage, c).start()
        else:

            @pl.when(middle_move)
            def _():
                o_ref[c] = landed[c]

            @pl.when(jnp.logical_not(middle_move))
            def _():
                o_ref[c] = final[c]

    early[first] = mix_ref[top, first]

    @pl.when(jnp.logical_not(ends_move))
    def _():
        w_last[...] = mix_ref[bits]

    stages = top + 5

    def step(t, carry):
        for stage in reversed(range(stages)):
            c = t - stage

            @pl.when((c >= 0) & (c < chunks))
            def _():
                task(stage, c)

        @pl.when(t == 0)
        def _():
            move_a.start()
            pl.when(ends_move)(move_b.start)

        @pl.when(t == 3)
        def _():
            move_a.wait_recv()
            w_top[last] = early[last]
            move_c.start()

        return carry

    lax.fori_loop(0, stages + chunks - 1, step, 0)

    def drain(c, carry):
        for stage in range(top + 3):
            transfer(stage, c).wait_send()
        pl.when(middle_move)(transfer(top + 3, c).wait_send)
        return carry

    lax.fori_loop(0, chunks, drain, 0)
    move_a.wait_send()
    pl.when(ends_move)(move_b.wait_send)
    move_c.wait_send()


def butterfly(sizes, coeffs, mix):
    chunks, _, k, width = coeffs.shape
    top = sum(size.bit_length() - 1 for size in sizes) - 1
    block = pltpu.VMEM(coeffs.shape, jnp.float32)
    weight = pltpu.VMEM((2, 2, k, k), jnp.float32)
    sems = pltpu.SemaphoreType.DMA((top + 4, chunks))
    w_sems = pltpu.SemaphoreType.DMA((3,))
    return pl.pallas_call(
        functools.partial(butterfly_kernel, sizes),
        out_shape=jax.ShapeDtypeStruct(coeffs.shape, jnp.float32),
        in_specs=[pl.BlockSpec(memory_space=pltpu.VMEM)] * 2,
        out_specs=pl.BlockSpec(memory_space=pltpu.VMEM),
        scratch_shapes=[block] * (2 * top + 6) + [weight] * 3 + [sems, sems, w_sems, w_sems],
        compiler_params=pltpu.CompilerParams(
            collective_id=0, has_side_effects=True, vmem_limit_bytes=60 * 2**20
        ),
    )(coeffs, mix)


def shards(right_sides, projector, mixing, expander):
    data = right_sides[:, 0]
    proj = projector[:, 0]
    mix = mixing[:, :, 0]
    sizes = tuple(lax.axis_size(name) for name in AXES)
    width = data.shape[2] // CHUNKS
    coeffs = jnp.stack(
        [
            jnp.einsum(
                "nlk,nlr->nkr",
                proj,
                data[:, :, i * width : (i + 1) * width],
                precision=lax.Precision.HIGHEST,
            )
            for i in range(CHUNKS)
        ]
    )
    return expand(expander, butterfly(sizes, coeffs, mix))


def solution(mesh):
    placed = (
        P(None, AXES, None, None),
        P(None, AXES, None, None),
        P(None, None, AXES, None, None, None),
        P(AXES, None, None),
    )
    return jax.shard_map(
        shards, mesh=mesh, in_specs=placed, out_specs=P(AXES, None, None), check_vma=False
    )
```

```python
import functools

import jax
import jax.numpy as jnp
from jax import lax
from jax.experimental import pallas as pl
from jax.experimental.pallas import tpu as pltpu
from jax.sharding import PartitionSpec as P

AXES = ("gx", "gy", "gz")
CHUNKS = 4


def split(x):
    hi = x.astype(jnp.bfloat16)
    lo = (x - hi.astype(jnp.float32)).astype(jnp.bfloat16)
    return hi, lo


def product(a, b):
    dot = functools.partial(jnp.dot, preferred_element_type=jnp.float32)
    return dot(a[0], b[0]) + (dot(a[0], b[1]) + dot(a[1], b[0]))


def expand_kernel(e_ref, c_ref, o_ref):
    o_ref[0] = product(split(e_ref[0]), split(c_ref[0, 0]))


def expand(expander, coeffs):
    nodes, leaf, k = expander.shape
    chunks, _, _, width = coeffs.shape
    return pl.pallas_call(
        expand_kernel,
        grid=(nodes, chunks),
        in_specs=[
            pl.BlockSpec((1, leaf, k), lambda n, c: (n, 0, 0)),
            pl.BlockSpec((1, 1, k, width), lambda n, c: (c, n, 0, 0)),
        ],
        out_specs=pl.BlockSpec((1, leaf, width), lambda n, c: (n, 0, c)),
        out_shape=jax.ShapeDtypeStruct((nodes, leaf, chunks * width), jnp.float32),
    )(expander, coeffs)


def butterfly_kernel(sizes, x_ref, mix_ref, early, o_ref, *scratch):
    bits = sum(size.bit_length() - 1 for size in sizes)
    top = bits - 1
    arrived = scratch[:top]
    values = (x_ref,) + tuple(scratch[top : 2 * top])
    (
        swap_a, swap_b, paired, swap_c, final, landed,
        w_top, w_last, send, recv, w_send, w_recv,
    ) = scratch[2 * top :]
    chunks = x_ref.shape[0]
    coords = [lax.axis_index(name) for name in AXES]
    me = (coords[0] * sizes[1] + coords[1]) * sizes[2] + coords[2]

    def bit_of(b):
        return (me // (1 << b)) % 2

    def place(d):
        return {
            "gx": d // (sizes[1] * sizes[2]),
            "gy": (d // sizes[2]) % sizes[1],
            "gz": d % sizes[2],
        }

    flips = [me + (1 - 2 * bit_of(b)) * (1 << b) for b in range(bits)]
    first, last = bit_of(0), bit_of(top)
    ends = me + (last - first) - (last - first) * (1 << top)
    middle = first + last * (1 << top)
    for b in range(1, top):
        middle = middle + bit_of(b) * (1 << (top - b))
    ends_move = first != last
    middle_move = middle != me

    def remote(src, dst, sems, index, target):
        return pltpu.make_async_remote_copy(
            src_ref=src,
            dst_ref=dst,
            send_sem=sems[0].at[index],
            recv_sem=sems[1].at[index],
            device_id=place(target),
            device_id_type=pl.DeviceIdType.MESH,
        )

    def transfer(stage, c):
        index = (stage, c)
        sems = (send, recv)
        if stage < top:
            return remote(values[stage].at[c], arrived[stage].at[c], sems, index, flips[stage])
        if stage == top:
            return remote(
                values[top].at[c, 1 - first], swap_a.at[c, first], sems, index, flips[0]
            )
        if stage == top + 1:
            return remote(swap_a.at[c, 1 - last], swap_b.at[c, last], sems, index, flips[top])
        if stage == top + 2:
            return remote(paired.at[c, 1 - first], swap_c.at[c, first], sems, index, flips[0])
        return remote(final.at[c], landed.at[c], sems, index, middle)

    w_sems = (w_send, w_recv)
    moves_b = [
        remote(mix_ref.at[bits, n, s], w_last.at[n, s], w_sems, 2 * n + s, ends)
        for n in range(2)
        for s in range(2)
    ]
    move_c = remote(early.at[1 - last], w_top.at[last], w_sems, 4, flips[top])

    def mixed(weights, own, other, out):
        parts = [split(own[n]) for n in range(2)]
        others = parts[::-1] if other is None else [split(other[n]) for n in range(2)]
        for n in range(2):
            out[n] = product(split(weights[n, 0]), parts[n]) + product(
                split(weights[n, 1]), others[n]
            )

    barrier = pltpu.get_barrier_semaphore()
    for target in flips:
        pl.semaphore_signal(
            barrier, inc=1, device_id=place(target), device_id_type=pl.DeviceIdType.MESH
        )
    for moves, target in ((ends_move, ends), (middle_move, middle)):

        @pl.when(moves)
        def _():
            pl.semaphore_signal(
                barrier, inc=1, device_id=place(target), device_id_type=pl.DeviceIdType.MESH
            )

    moving = ends_move.astype(jnp.int32) + middle_move.astype(jnp.int32)
    pl.semaphore_wait(barrier, len(flips) + moving)

    def task(stage, c):
        if stage > 0:
            before = transfer(stage - 1, c)
            if stage - 1 == top + 3:
                pl.when(middle_move)(before.wait_recv)
            else:
                before.wait_recv()
        if 0 < stage <= top:
            mixed(
                mix_ref.at[stage - 1],
                values[stage - 1].at[c],
                arrived[stage - 1].at[c],
                values[stage].at[c],
            )
        if stage == top:
            swap_a[c, first] = values[top][c, first]
        if stage == top + 1:
            swap_b[c, last] = swap_a[c, last]
        if stage == top + 2:

            @pl.when(c == 0)
            def _():
                move_c.wait_recv()

            mixed(w_top, swap_b.at[c], None, paired.at[c])
            swap_c[c, first] = paired[c, first]
        if stage == top + 3:

            @pl.when((c == 0) & ends_move)
            def _():
                for move in moves_b:
                    move.wait_recv()

            mixed(w_last, swap_c.at[c], None, final.at[c])
            pl.when(middle_move)(transfer(stage, c).start)
        elif stage < top + 3:
            transfer(stage, c).start()
        else:

            @pl.when(middle_move)
            def _():
                o_ref[c] = landed[c]

            @pl.when(jnp.logical_not(middle_move))
            def _():
                o_ref[c] = final[c]

    w_top[last] = early[last]

    @pl.when(jnp.logical_not(ends_move))
    def _():
        w_last[...] = mix_ref[bits]

    stages = top + 5

    def step(t, carry):
        for stage in reversed(range(1, stages)):
            c = t - stage

            @pl.when((c >= 0) & (c < chunks))
            def _():
                task(stage, c)

        @pl.when(t + 1 < chunks)
        def _():
            task(0, t + 1)

        for i, move in enumerate(moves_b):
            pl.when((t == i) & ends_move)(move.start)

        return carry

    move_c.start()
    task(0, 0)
    lax.fori_loop(0, stages + chunks - 1, step, 0)

    def drain(c, carry):
        for stage in range(top + 3):
            transfer(stage, c).wait_send()
        pl.when(middle_move)(transfer(top + 3, c).wait_send)
        return carry

    lax.fori_loop(0, chunks, drain, 0)
    for move in moves_b:
        pl.when(ends_move)(move.wait_send)
    move_c.wait_send()


def butterfly(sizes, coeffs, mix, early):
    chunks, _, k, width = coeffs.shape
    top = sum(size.bit_length() - 1 for size in sizes) - 1
    block = pltpu.VMEM(coeffs.shape, jnp.float32)
    weight = pltpu.VMEM((2, 2, k, k), jnp.float32)
    sems = pltpu.SemaphoreType.DMA((top + 4, chunks))
    w_sems = pltpu.SemaphoreType.DMA((5,))
    return pl.pallas_call(
        functools.partial(butterfly_kernel, sizes),
        out_shape=jax.ShapeDtypeStruct(coeffs.shape, jnp.float32),
        in_specs=[pl.BlockSpec(memory_space=pltpu.VMEM)] * 3,
        out_specs=pl.BlockSpec(memory_space=pltpu.VMEM),
        scratch_shapes=[block] * (2 * top + 6) + [weight] * 2 + [sems, sems, w_sems, w_sems],
        compiler_params=pltpu.CompilerParams(
            collective_id=0, has_side_effects=True, vmem_limit_bytes=60 * 2**20
        ),
    )(coeffs, mix, early)


def shards(right_sides, projector, mixing, expander):
    data = right_sides[:, 0]
    proj = projector[:, 0]
    mix = mixing[:, :, 0]
    sizes = tuple(lax.axis_size(name) for name in AXES)
    width = data.shape[2] // CHUNKS
    coeffs = jnp.stack(
        [
            jnp.einsum(
                "nlk,nlr->nkr",
                proj,
                data[:, :, i * width : (i + 1) * width],
                precision=lax.Precision.HIGHEST,
            )
            for i in range(CHUNKS)
        ]
    )
    total = lax.axis_size(AXES)
    outer = mix[mix.shape[0] - 2]
    own_zero = lax.axis_index(AXES) % 2 == 0
    arrived = lax.ppermute(
        jnp.where(own_zero, outer[1], outer[0]), AXES, [(d, d ^ 1) for d in range(total)]
    )
    early = jnp.stack(
        [jnp.where(own_zero, outer[0], arrived), jnp.where(own_zero, arrived, outer[1])]
    )
    return expand(expander, butterfly(sizes, coeffs, mix, early))


def solution(mesh):
    placed = (
        P(None, AXES, None, None),
        P(None, AXES, None, None),
        P(None, None, AXES, None, None, None),
        P(AXES, None, None),
    )
    return jax.shard_map(
        shards, mesh=mesh, in_specs=placed, out_specs=P(AXES, None, None), check_vma=False
    )
```
